32 devices in a mesh: grp: 8 (over z, x), mem: 4 (over y, core).
Axes of the slice: x: 2, y: 2, z: 4, core: 2. Of those that a mesh axis runs over, the one named last changes fastest.
Arguments:
- right_side: float32 [32, 65536], P(None, ('grp', 'mem')), may hold values from -6 to 6
- fine_tiles: float32 [512, 3, 128, 128], P(('grp', 'mem')), may hold values from -0.13492627 to 6.130239
- fine_columns: int32 [512, 3], P(('grp', 'mem')), may hold values from 0 to 19, as said below
- fine_sends: int32 [64, 256], P(('grp', 'mem')), may hold values from 0 to 2047, as said below
- fine_weights: float32 [65536], P(('grp', 'mem')), may hold values from 0.5 to 2
- fine_groups: int32 [65536], P(('grp', 'mem')), may hold values from 0 to 255, as said below
- group_tiles: float32 [64, 3, 128, 128], P('grp'), may hold values from -1.0794102 to 49.0419102
- group_columns: int32 [64, 3], P('grp'), may hold values from 0 to 9, as said below
- group_sends: int32 [16, 128], P('grp'), may hold values from 0 to 1023, as said below
- group_weights: float32 [8192], P('grp'), may hold values from 0.5 to 2
- group_groups: int32 [8192], P('grp'), may hold values from 0 to 31, as said below
- coarse_tiles: float32 [2, 3, 128, 128], replicated, may hold values from -2.1588203 to 98.08382034355964
- coarse_columns: int32 [2, 3], replicated, may hold values from 0 to 1, as said below
Outputs:
- solution: float32 [32, 65536], P(None, ('grp', 'mem'))
- residual: float32 [32, 65536], P(None, ('grp', 'mem'))
The draws below stay inside these ranges and needn't reach their ends.
Inputs may be any that keep to these rules, and one draw needn't show every extreme that they name: `fine_columns`: fine tiles: within each owner's 16 tile rows, entry 0 is the tile row's own index; entries 1 each name a distinct block of the extended vector (16 own blocks, then 2 from the lower neighbour, then 2 from the higher), and so do entries 2; every halo block is named by entries 2. `fine_sends`: each list holds 256 distinct rows of its owner; list 2 o goes to owner o - 1, list 2 o + 1 to owner o + 1. `fine_groups`: each aggregate of an owner takes exactly 8 of its rows. `group_columns`: as for fine_columns, per group, with 8 tile rows and 2 halo blocks. `group_sends`: each list holds 128 distinct rows of its group. `group_groups`: each aggregate of a group takes exactly 32 of its rows. `coarse_columns`: entry 0 is the tile row's own index; entries 1 name each block once, and so do entries 2.
All inputs are finite; a program needn't handle non-finite values.
Results may differ from the reference program's by a relative error of at most 0.0003.
Values sent between devices are 32-bit elements; how exact they have to be, the bound alone decides.
A program may use at most 128 MiB of HBM per device.

```python
import functools
import math
import jax
import jax.numpy as jnp
from jax import lax

NRHS = 32
R0 = 2048
TILE = 128
HALO0 = 256
HALO1 = 128
AGG1 = 8
AGG2 = 32
ITERS = 2
NB0 = 16
HB0 = 4
ROWS1 = 1024
NB1 = 8
HB1 = 2
ROWS2 = 32
COARSE = 256
NB2 = 2
UNKNOWNS = 65536
N_GRP = 8
N_MEM = 4


PULL = 0.15


ROUGH = 0.25


def tile_block(key, block_count, scale):
    entry_key, boost_key = jax.random.split(key)
    reach = 3 * TILE
    entries = jax.random.uniform(entry_key, (block_count, 3, TILE, TILE), jnp.float32, -1.0, 1.0)
    entries = ROUGH * (3.0 / reach) ** 0.5 * entries - PULL / reach
    boost = jax.random.uniform(boost_key, (block_count, TILE), jnp.float32, 3.0, 6.0)
    entries = boost[:, None, :, None] * entries
    identity = jnp.eye(TILE, dtype=jnp.float32)
    entries = entries.at[:, 0].add(boost[:, :, None] * identity[None])
    return scale * entries


def column_block(key, block_count, halo_blocks):
    first_key, second_key, place_key = jax.random.split(key, 3)
    own_index = jnp.arange(block_count, dtype=jnp.int32)
    first_col = jax.random.permutation(first_key, block_count + halo_blocks)[:block_count].astype(jnp.int32)
    second_col = jax.random.permutation(second_key, block_count).astype(jnp.int32)
    if halo_blocks > 0:
        positions = jax.random.permutation(place_key, block_count)[:halo_blocks]
        second_col = second_col.at[positions].set(block_count + jnp.arange(halo_blocks, dtype=jnp.int32))
    return jnp.stack([own_index, first_col, second_col], axis=1)


def send_block(key, row_count, list_length):
    return jax.random.permutation(key, row_count)[:list_length].astype(jnp.int32)


def group_block(key, row_count, group_size):
    return (jax.random.permutation(key, row_count) // group_size).astype(jnp.int32)


def draw_right_side(key, part):
    normal_part = jax.random.normal(jax.random.fold_in(key, 11), (NRHS, R0 * N_GRP * N_MEM), jnp.float32)
    return jnp.clip(normal_part, -6.0, 6.0)


def draw_fine_tiles(key, part):
    return tile_block(jax.random.fold_in(key, 21), NB0 * N_GRP * N_MEM, 1.0)


def draw_group_tiles(key, part):
    return tile_block(jax.random.fold_in(key, 22), NB1 * N_GRP, 1.0 * AGG1)


def draw_coarse_tiles(key, part):
    return tile_block(jax.random.fold_in(key, 23), NB2, (1.0 * AGG1 * AGG2) ** 0.5)


def draw_fine_columns(key, part):
    key_list = jax.random.split(jax.random.fold_in(key, 31), N_GRP * N_MEM)
    return jax.vmap(lambda subkey: column_block(subkey, NB0, HB0))(key_list).reshape(-1, 3)


def draw_group_columns(key, part):
    key_list = jax.random.split(jax.random.fold_in(key, 32), N_GRP)
    return jax.vmap(lambda subkey: column_block(subkey, NB1, HB1))(key_list).reshape(-1, 3)


def draw_coarse_columns(key, part):
    return column_block(jax.random.fold_in(key, 33), NB2, 0)


def draw_fine_sends(key, part):
    key_list = jax.random.split(jax.random.fold_in(key, 41), 2 * N_GRP * N_MEM)
    return jax.vmap(lambda subkey: send_block(subkey, R0, HALO0))(key_list)


def draw_group_sends(key, part):
    key_list = jax.random.split(jax.random.fold_in(key, 42), 2 * N_GRP)
    return jax.vmap(lambda subkey: send_block(subkey, ROWS1, HALO1))(key_list)


def draw_fine_groups(key, part):
    key_list = jax.random.split(jax.random.fold_in(key, 51), N_GRP * N_MEM)
    return jax.vmap(lambda subkey: group_block(subkey, R0, AGG1))(key_list).reshape(-1)


def draw_group_groups(key, part):
    key_list = jax.random.split(jax.random.fold_in(key, 52), N_GRP)
    return jax.vmap(lambda subkey: group_block(subkey, ROWS1, AGG2))(key_list).reshape(-1)


def shard_levels(key, extent, cuts, least, largest):
    def one(position, shards_of):
        draws = jax.random.uniform(jax.random.fold_in(jax.random.fold_in(key, 6), position), (shards_of,), jnp.float32, least / len(cuts), largest / len(cuts))
        return jnp.repeat(jnp.exp(draws), extent[position] // shards_of).reshape((-1,) + (1,) * (len(extent) - position - 1))

    level = one(*cuts[0])
    for cut in cuts[1:]:
        level = level * one(*cut)
    return level


def setup_inputs(seed: int = 0) -> dict:
    keys = jax.random.split(jax.random.key(seed), 14)
    return {
        "right_side": draw_right_side(jax.random.fold_in(keys[13], 71), 0),
        "fine_tiles": draw_fine_tiles(jax.random.fold_in(keys[13], 71), 0),
        "fine_columns": draw_fine_columns(jax.random.fold_in(keys[13], 71), 0),
        "fine_sends": draw_fine_sends(jax.random.fold_in(keys[13], 71), 0),
        "fine_weights": jnp.clip(jnp.exp(math.log(2.0) - 1.3862944 * jax.random.uniform(keys[4], (UNKNOWNS,), jnp.float32) ** shard_levels(keys[4], (UNKNOWNS,), ((0, 32),), -0.2, 0.2)), 0.5, 2.0),
        "fine_groups": draw_fine_groups(jax.random.fold_in(keys[13], 71), 0),
        "group_tiles": draw_group_tiles(jax.random.fold_in(keys[13], 71), 0),
        "group_columns": draw_group_columns(jax.random.fold_in(keys[13], 71), 0),
        "group_sends": draw_group_sends(jax.random.fold_in(keys[13], 71), 0),
        "group_weights": jnp.clip(jnp.exp(math.log(2.0) - 1.3862944 * jax.random.uniform(keys[9], (ROWS1 * N_GRP,), jnp.float32) ** shard_levels(keys[9], (ROWS1 * N_GRP,), ((0, 8),), -0.2, 0.2)), 0.5, 2.0),
        "group_groups": draw_group_groups(jax.random.fold_in(keys[13], 71), 0),
        "coarse_tiles": draw_coarse_tiles(jax.random.fold_in(keys[13], 71), 0),
        "coarse_columns": draw_coarse_columns(jax.random.fold_in(keys[13], 71), 0),
    }


RELAXATION = 0.7


def tile_apply(tile_set, tile_cols, extended):
    tile_width = tile_set.shape[2]
    blocks = extended.reshape(extended.shape[0], -1, tile_width)
    picked = blocks[:, tile_cols, :]
    result = jnp.einsum("bkij,nbkj->nbi", tile_set, picked, precision=lax.Precision.HIGHEST)
    return result.reshape(extended.shape[0], -1)


def scaled_inverse(tile_set, tile_cols):
    block_count = tile_set.shape[0]
    own_mask = (tile_cols == jnp.arange(block_count, dtype=jnp.int32)[:, None]).astype(tile_set.dtype)
    diagonal = jnp.sum(own_mask[:, :, None] * jnp.diagonal(tile_set, axis1=2, axis2=3), axis=1)
    return (RELAXATION / diagonal).reshape(-1)


def pick_rows(vector, row_index):
    return vector[:, row_index]


def owner_extend(values, send_lists):
    to_lower = jax.vmap(pick_rows)(values, send_lists[:, 0])
    to_upper = jax.vmap(pick_rows)(values, send_lists[:, 1])
    nothing = jnp.zeros_like(to_lower[:1])
    from_lower = jnp.concatenate([nothing, to_upper[:-1]], axis=0)
    from_upper = jnp.concatenate([to_lower[1:], nothing], axis=0)
    return jnp.concatenate([values, from_lower, from_upper], axis=2)


def restrict_rows(values, weights, agg_map, coarse_count):
    return jax.ops.segment_sum((values * weights).T, agg_map, coarse_count).T


def prolong_rows(values, weights, agg_map):
    return weights * values[:, agg_map]


def inner_sum(first_vec, second_vec):
    return jnp.sum(first_vec * second_vec, axis=(0, 2))


def reference(right_side, fine_tiles, fine_columns, fine_sends, fine_weights, fine_groups,
              group_tiles, group_columns, group_sends, group_weights, group_groups,
              coarse_tiles, coarse_columns):
    owners = N_GRP * N_MEM
    fine_count = R0 // AGG1
    fine_set = fine_tiles.reshape(owners, NB0, 3, TILE, TILE)
    fine_cols = fine_columns.reshape(owners, NB0, 3)
    fine_lists = fine_sends.reshape(owners, 2, HALO0)
    fine_wts = fine_weights.reshape(owners, R0)
    fine_maps = fine_groups.reshape(owners, R0)
    group_set = group_tiles.reshape(N_GRP, NB1, 3, TILE, TILE)
    group_cols = group_columns.reshape(N_GRP, NB1, 3)
    group_lists = group_sends.reshape(N_GRP, 2, HALO1)
    group_wts = group_weights.reshape(N_GRP, ROWS1)
    group_maps = group_groups.reshape(N_GRP, ROWS1)
    fine_scale = jax.vmap(scaled_inverse)(fine_set, fine_cols)[:, None, :]
    group_scale = jax.vmap(scaled_inverse)(group_set, group_cols)[:, None, :]
    coarse_scale = scaled_inverse(coarse_tiles, coarse_columns)
    fine_restrict = jax.vmap(functools.partial(restrict_rows, coarse_count=fine_count))
    group_restrict = jax.vmap(functools.partial(restrict_rows, coarse_count=ROWS2))

    def fine_apply(values):
        return jax.vmap(tile_apply)(fine_set, fine_cols, owner_extend(values, fine_lists))

    def group_apply(values):
        return jax.vmap(tile_apply)(group_set, group_cols, owner_extend(values, group_lists))

    def vcycle(source):
        fine_iter = fine_scale * source
        fine_left = source - fine_apply(fine_iter)
        lowered = fine_restrict(fine_left, fine_wts, fine_maps)
        group_rhs = lowered.reshape(N_GRP, N_MEM, NRHS, fine_count).transpose(0, 2, 1, 3).reshape(N_GRP, NRHS, ROWS1)
        group_iter = group_scale * group_rhs
        group_left = group_rhs - group_apply(group_iter)
        coarse_part = group_restrict(group_left, group_wts, group_maps)
        coarse_rhs = coarse_part.transpose(1, 0, 2).reshape(NRHS, COARSE)
        coarse_iter = coarse_scale * coarse_rhs
        coarse_iter = coarse_iter + coarse_scale * (coarse_rhs - tile_apply(coarse_tiles, coarse_columns, coarse_iter))
        raised = coarse_iter.reshape(NRHS, N_GRP, ROWS2).transpose(1, 0, 2)
        group_iter = group_iter + jax.vmap(prolong_rows)(raised, group_wts, group_maps)
        group_iter = group_iter + group_scale * (group_rhs - group_apply(group_iter))
        spread = group_iter.reshape(N_GRP, NRHS, N_MEM, fine_count).transpose(0, 2, 1, 3).reshape(owners, NRHS, fine_count)
        fine_iter = fine_iter + jax.vmap(prolong_rows)(spread, fine_wts, fine_maps)
        return fine_iter + fine_scale * (source - fine_apply(fine_iter))

    residual = right_side.reshape(NRHS, owners, R0).transpose(1, 0, 2)
    solution = jnp.zeros_like(residual)
    precond = vcycle(residual)
    energy = inner_sum(residual, precond)
    direction = precond
    for iteration in range(ITERS):
        images = fine_apply(direction)
        step_size = (energy / inner_sum(direction, images))[None, :, None]
        solution = solution + step_size * direction
        residual = residual - step_size * images
        if iteration + 1 < ITERS:
            precond = vcycle(residual)
            fresh = inner_sum(residual, precond)
            direction = precond + (fresh / energy)[None, :, None] * direction
            energy = fresh
    solution = solution.transpose(1, 0, 2).reshape(NRHS, UNKNOWNS)
    residual = residual.transpose(1, 0, 2).reshape(NRHS, UNKNOWNS)
    return solution, residual
```

```python
import functools

import jax
import jax.numpy as jnp
from jax import lax
from jax.experimental import pallas as pl
from jax.experimental.pallas import tpu as pltpu
from jax.sharding import PartitionSpec as P

ITERS = 2
RELAXATION = 0.7
AGG1 = 8
AGG2 = 32
F32, BF16 = jnp.float32, jnp.bfloat16
MESH = pl.DeviceIdType.MESH


def high_part(x):
    return x.astype(BF16)


def low_part(x):
    return (x - x.astype(BF16).astype(F32)).astype(BF16)


def split(x):
    return jnp.concatenate([high_part(x), low_part(x)], axis=0)


def joined(y):
    half = y.shape[0] // 2
    return y[:half] + y[half:]


def mm(x, w):
    return joined(jnp.dot(split(x), w, preferred_element_type=F32))


def dot_nt(x, w):
    return lax.dot_general(x, w, (((1,), (1,)), ((), ())), preferred_element_type=F32)


def mm_nt(x, w):
    return joined(dot_nt(split(x), w))


def iota(shape, dim):
    return lax.broadcasted_iota(jnp.int32, shape, dim)


def kernel(
    ng, nm,
    fcols, gcols, ccols,
    rhs, ftiles, fsends, fweights, fgroups,
    gtiles, gsends, gweights, ggroups, ctiles,
    sol_out, res_out,
    fhi, flo, ghi, glo, chi, clo,
    fscale, gscale, cscale,
    fsel, gsel, fagg, gagg,
    fext, gext, cext,
    fy, gy, cy,
    x0, x1, zed, img,
    fout, fin, gout, gin, gathered, cparts, sums_m, sums_g,
    fs_send, fs_recv, gs_send, gs_recv, ag_send, ag_recv, cg_send, cg_recv,
    sm_send, sm_recv, sg_send, sg_recv,
):
    grp, mem = lax.axis_index("grp"), lax.axis_index("mem")
    me = grp * nm + mem
    T = ftiles.shape[-1]
    nrhs = rhs.shape[0]
    nb0, nb1, nb2 = ftiles.shape[0], gtiles.shape[0], ctiles.shape[0]
    rows0, rows1, rows2 = nb0 * T, nb1 * T, nb2 * T
    halo0, halo1 = fsends.shape[1] // 2, gsends.shape[1] // 2
    h0, h1 = halo0 // T, halo1 // T
    own1 = rows0 // AGG1
    ob1 = own1 // T
    share = rows1 // AGG2
    place = lax.rem(grp * share, T)
    cblock = lax.div(grp * share, T)

    has_lower, has_upper = me > 0, me < ng * nm - 1
    low_id = jnp.maximum(me - 1, 0)
    up_id = jnp.minimum(me + 1, ng * nm - 1)
    lower = (lax.div(low_id, nm), lax.rem(low_id, nm))
    upper = (lax.div(up_id, nm), lax.rem(up_id, nm))
    g_lower, g_upper = grp > 0, grp < ng - 1
    lower_g = (jnp.maximum(grp - 1, 0), mem)
    upper_g = (jnp.minimum(grp + 1, ng - 1), mem)

    fin[...] = jnp.zeros_like(fin)
    gin[...] = jnp.zeros_like(gin)

    barrier = pltpu.get_barrier_semaphore()
    for d in range(1, nm):
        pl.semaphore_signal(barrier, inc=1, device_id=(grp, lax.rem(mem + d, nm)), device_id_type=MESH)
    for d in range(1, ng):
        pl.semaphore_signal(barrier, inc=1, device_id=(lax.rem(grp + d, ng), mem), device_id_type=MESH)

    @pl.when(has_lower)
    def _():
        pl.semaphore_signal(barrier, inc=1, device_id=lower, device_id_type=MESH)

    @pl.when(has_upper)
    def _():
        pl.semaphore_signal(barrier, inc=1, device_id=upper, device_id_type=MESH)

    eye = iota((T, T), 0) == iota((T, T), 1)

    def prepare(tiles, cols, hi, lo, scale, count):
        @pl.loop(0, count)
        def _(b):
            diagonal = jnp.zeros((1, T), F32)
            for k in range(3):
                t = tiles[b, k]
                d = jnp.sum(jnp.where(eye, t, 0.0), axis=0, keepdims=True)
                diagonal = diagonal + jnp.where(cols[b, k] == b, 1.0, 0.0) * d
                hi[b, :, k * T : (k + 1) * T] = high_part(t)
                lo[b, :, k * T : (k + 1) * T] = low_part(t)
            scale[:, pl.ds(pl.multiple_of(b * T, T), T)] = RELAXATION / diagonal

    prepare(ftiles, fcols, fhi, flo, fscale, nb0)

    def one_hot_rows(sel, lists, count):
        width = lists.shape[1]

        @pl.loop(0, count)
        def _(b):
            at = pl.multiple_of(b * T, T)
            sel[pl.ds(at, T), :] = jnp.where(iota((T, width), 0) + at == lists[...], 1.0, 0.0).astype(BF16)

    one_hot_rows(fsel, fsends, nb0)

    pl.semaphore_wait(
        barrier, nm - 1 + ng - 1 + has_lower.astype(jnp.int32) + has_upper.astype(jnp.int32)
    )

    def halo_pair(out, into, send, recv, h, slot, low_dev, up_dev):
        def copy(side, dev):
            return pltpu.make_async_remote_copy(
                src_ref=out.at[slot, pl.ds(side * h, h)],
                dst_ref=into.at[slot, pl.ds((1 - side) * h, h)],
                send_sem=send.at[slot, side],
                recv_sem=recv.at[slot, 1 - side],
                device_id=dev,
                device_id_type=MESH,
            )

        return copy(0, low_dev), copy(1, up_dev)

    def f_pair(slot):
        return halo_pair(fout, fin, fs_send, fs_recv, h0, slot, lower, upper)

    def g_pair(slot):
        return halo_pair(gout, gin, gs_send, gs_recv, h1, slot, lower_g, upper_g)

    def start(pair, low, up):
        @pl.when(low)
        def _():
            pair[0].start()

        @pl.when(up)
        def _():
            pair[1].start()

    def finish(pair, low, up):
        @pl.when(low)
        def _():
            pair[0].wait_send()
            pair[1].wait_recv()

        @pl.when(up)
        def _():
            pair[1].wait_send()
            pair[0].wait_recv()

    def fine_send(x, slot):
        picked = mm(x, fsel[...])
        for s in range(2 * h0):
            fout[slot, s] = picked[:, s * T : (s + 1) * T]
        start(f_pair(slot), has_lower, has_upper)

    def group_send(x, slot):
        picked = mm(x, gsel[...])
        for s in range(2 * h1):
            gout[slot, s] = picked[:, s * T : (s + 1) * T]
        start(g_pair(slot), g_lower, g_upper)

    def put_own(x, ext, count):
        parts = split(x)
        for b in range(count):
            ext[b] = parts[:, b * T : (b + 1) * T]

    def apply(ext, cols, hi, lo, y, count):
        step = 4 if count % 4 == 0 else (2 if count % 2 == 0 else 1)

        @pl.loop(0, count // step)
        def _(i):
            for j in range(step):
                b = i * step + j
                xs = jnp.concatenate([ext[cols[b, k]] for k in range(3)], axis=1)
                r = joined(dot_nt(xs, hi[b])) + dot_nt(xs[:nrhs], lo[b])
                y[:, pl.ds(pl.multiple_of(b * T, T), T)] = r

    def fine_apply(slot):
        finish(f_pair(slot), has_lower, has_upper)
        for s in range(2 * h0):
            fext[nb0 + s] = split(fin[slot, s])
        apply(fext, fcols, fhi, flo, fy, nb0)
        return fy[...]

    def group_apply(slot):
        finish(g_pair(slot), g_lower, g_upper)
        for s in range(2 * h1):
            gext[nb1 + s] = split(gin[slot, s])
        apply(gext, gcols, ghi, glo, gy, nb1)
        return gy[...]

    def spread_copies(buf, it, mine, size, send, recv, axis):
        n = nm if axis == "mem" else ng
        out = []
        for d in range(1, n):
            dev = (grp, lax.rem(mem + d, nm)) if axis == "mem" else (lax.rem(grp + d, ng), mem)
            ref = buf.at[it, pl.ds(mine * size, size)]
            out.append(
                pltpu.make_async_remote_copy(
                    src_ref=ref, dst_ref=ref,
                    send_sem=send.at[it, d - 1], recv_sem=recv.at[it, d - 1],
                    device_id=dev, device_id_type=MESH,
                )
            )
        return out

    def run(copies):
        for c in copies:
            c.start()
        for c in copies:
            c.wait()

    def reduced(quantities, it):
        lanes = iota((8, T), 1)
        packed = jnp.zeros((8, T), F32)
        groups = nrhs // 8
        nq = len(quantities)
        for q, (a, b) in enumerate(quantities):
            s = jnp.sum(a * b, axis=1, keepdims=True)
            for k in range(groups):
                packed = jnp.where(lanes == k * nq + q, s[8 * k : 8 * k + 8], packed)
        sums_m[it, mem] = packed
        run(spread_copies(sums_m, it, mem, 1, sm_send, sm_recv, "mem"))
        total = sums_m[it, 0]
        for m in range(1, nm):
            total = total + sums_m[it, m]
        sums_g[it, grp] = total
        run(spread_copies(sums_g, it, grp, 1, sg_send, sg_recv, "grp"))
        total = sums_g[it, 0]
        for g in range(1, ng):
            total = total + sums_g[it, g]
        return [
            jnp.concatenate([total[:, k * nq + q : k * nq + q + 1] for k in range(groups)], axis=0)
            for q in range(nq)
        ]

    res_out[...] = rhs[...]
    start_x = fscale[...] * rhs[...]
    fine_send(start_x, 0)
    put_own(start_x, fext, nb0)
    x0[...] = start_x

    fagg[...] = jnp.where(iota((own1, rows0), 0) == fgroups[...], 1.0, 0.0).astype(BF16)
    gagg[...] = jnp.where(iota((T, rows1), 0) == ggroups[...] + place, 1.0, 0.0).astype(BF16)
    prepare(gtiles, gcols, ghi, glo, gscale, nb1)
    prepare(ctiles, ccols, chi, clo, cscale, nb2)
    one_hot_rows(gsel, gsends, nb1)

    for it in range(ITERS):
        base, gbase = 3 * it, 2 * it
        left = res_out[...] - (fine_apply(base) if it == 0 else fy[...])
        lowered = mm_nt(left * fweights[...], fagg[...])
        for s in range(ob1):
            gathered[it, mem * ob1 + s] = lowered[:, s * T : (s + 1) * T]
        run(spread_copies(gathered, it, mem, ob1, ag_send, ag_recv, "mem"))
        b1 = jnp.concatenate([gathered[it, b] for b in range(nb1)], axis=1)
        first = gscale[...] * b1
        group_send(first, gbase)
        put_own(first, gext, nb1)
        left = b1 - group_apply(gbase)
        cparts[it, grp] = mm_nt(left * gweights[...], gagg[...])
        run(spread_copies(cparts, it, grp, 1, cg_send, cg_recv, "grp"))
        per = T // share
        blocks = []
        for c in range(nb2):
            total = cparts[it, c * per]
            for g in range(c * per + 1, (c + 1) * per):
                total = total + cparts[it, g]
            blocks.append(total)
        b2 = jnp.concatenate(blocks, axis=1)
        x2 = cscale[...] * b2
        put_own(x2, cext, nb2)
        apply(cext, ccols, chi, clo, cy, nb2)
        cy[...] = x2 + cscale[...] * (b2 - cy[...])
        raised = cy[:, pl.ds(pl.multiple_of(cblock * T, T), T)]
        x1v = first + gweights[...] * mm(raised, gagg[...])
        group_send(x1v, gbase + 1)
        put_own(x1v, gext, nb1)
        x1[...] = x1v + gscale[...] * (b1 - group_apply(gbase + 1))
        mine = x1[:, pl.ds(pl.multiple_of(mem * own1, T), own1)]
        x0v = x0[...] + fweights[...] * mm(mine, fagg[...])
        fine_send(x0v, base + 1)
        put_own(x0v, fext, nb0)
        z = x0v + fscale[...] * (res_out[...] - fine_apply(base + 1))
        fine_send(z, base + 2)
        put_own(z, fext, nb0)
        q = fine_apply(base + 2)
        if it == 0:
            zed[...] = z
            img[...] = q
            fine_send(fscale[...] * q, base + 3)
            energy, curvature = reduced([(res_out[...], z), (z, q)], it)
            step = energy / curvature
            sol_out[...] = step * zed[...]
            res = res_out[...] - step * img[...]
            res_out[...] = res
            x0v = fscale[...] * res
            x0[...] = x0v
            put_own(x0v, fext, nb0)
            finish(f_pair(base + 3), has_lower, has_upper)
            for s in range(2 * h0):
                fext[nb0 + s] = split(fin[0, s] - step * fin[base + 3, s])
            apply(fext, fcols, fhi, flo, fy, nb0)
        else:
            fresh, own, one, two = reduced(
                [(res_out[...], z), (z, q), (z, img[...]), (zed[...], q)], it
            )
            ratio = fresh / energy
            curvature = own + ratio * (one + two) + ratio * ratio * curvature
            step = fresh / curvature
            sol_out[...] = sol_out[...] + step * (z + ratio * zed[...])
            res_out[...] = res_out[...] - step * (q + ratio * img[...])


def shards(
    ng, nm,
    right_side, fine_tiles, fine_columns, fine_sends, fine_weights, fine_groups,
    group_tiles, group_columns, group_sends, group_weights, group_groups,
    coarse_tiles, coarse_columns,
):
    nrhs, rows0 = right_side.shape
    T = fine_tiles.shape[-1]
    nb0, nb1, nb2 = fine_tiles.shape[0], group_tiles.shape[0], coarse_tiles.shape[0]
    rows1, rows2 = nb1 * T, nb2 * T
    h0, h1 = fine_sends.shape[1] // T, group_sends.shape[1] // T
    own1 = rows0 // AGG1
    vm, dma = pltpu.VMEM, pltpu.SemaphoreType.DMA
    scratch = [
        vm((nb0, T, 3 * T), BF16), vm((nb0, T, 3 * T), BF16),
        vm((nb1, T, 3 * T), BF16), vm((nb1, T, 3 * T), BF16),
        vm((nb2, T, 3 * T), BF16), vm((nb2, T, 3 * T), BF16),
        vm((1, rows0), F32), vm((1, rows1), F32), vm((1, rows2), F32),
        vm((rows0, 2 * h0 * T), BF16), vm((rows1, 2 * h1 * T), BF16),
        vm((own1, rows0), BF16), vm((T, rows1), BF16),
        vm((nb0 + 2 * h0, 2 * nrhs, T), BF16),
        vm((nb1 + 2 * h1, 2 * nrhs, T), BF16),
        vm((nb2, 2 * nrhs, T), BF16),
        vm((nrhs, rows0), F32), vm((nrhs, rows1), F32), vm((nrhs, rows2), F32),
        vm((nrhs, rows0), F32), vm((nrhs, rows1), F32),
        vm((nrhs, rows0), F32), vm((nrhs, rows0), F32),
        vm((3 * ITERS, 2 * h0, nrhs, T), F32), vm((3 * ITERS, 2 * h0, nrhs, T), F32),
        vm((2 * ITERS, 2 * h1, nrhs, T), F32), vm((2 * ITERS, 2 * h1, nrhs, T), F32),
        vm((ITERS, nb1, nrhs, T), F32), vm((ITERS, ng, nrhs, T), F32),
        vm((ITERS, nm, 8, T), F32), vm((ITERS, ng, 8, T), F32),
        dma((3 * ITERS, 2)), dma((3 * ITERS, 2)),
        dma((2 * ITERS, 2)), dma((2 * ITERS, 2)),
        dma((ITERS, nm - 1)), dma((ITERS, nm - 1)),
        dma((ITERS, ng - 1)), dma((ITERS, ng - 1)),
        dma((ITERS, nm - 1)), dma((ITERS, nm - 1)),
        dma((ITERS, ng - 1)), dma((ITERS, ng - 1)),
    ]
    in_vm, in_sm = pl.BlockSpec(memory_space=pltpu.VMEM), pl.BlockSpec(memory_space=pltpu.SMEM)
    out = jax.ShapeDtypeStruct((nrhs, rows0), F32)
    return pl.pallas_call(
        functools.partial(kernel, ng, nm),
        out_shape=(out, out),
        in_specs=[in_sm] * 3 + [in_vm] * 10,
        out_specs=(in_vm, in_vm),
        scratch_shapes=scratch,
        compiler_params=pltpu.CompilerParams(
            collective_id=0, has_side_effects=True, vmem_limit_bytes=60 << 20
        ),
    )(
        fine_columns, group_columns, coarse_columns,
        right_side, fine_tiles, fine_sends.reshape(1, -1), fine_weights.reshape(1, -1),
        fine_groups.reshape(1, -1), group_tiles, group_sends.reshape(1, -1),
        group_weights.reshape(1, -1), group_groups.reshape(1, -1), coarse_tiles,
    )


def solution(mesh):
    both = ("grp", "mem")
    return jax.shard_map(
        functools.partial(shards, mesh.shape["grp"], mesh.shape["mem"]),
        mesh=mesh,
        in_specs=(
            P(None, both), P(both, None, None, None), P(both, None), P(both, None), P(both), P(both),
            P("grp", None, None, None), P("grp", None), P("grp", None), P("grp"), P("grp"),
            P(), P(),
        ),
        out_specs=(P(None, both), P(None, both)),
        check_vma=False,
    )
```

```python
import functools

import jax
import jax.numpy as jnp
from jax import lax
from jax.experimental import pallas as pl
from jax.experimental.pallas import tpu as pltpu
from jax.sharding import PartitionSpec as P

ITERS = 2
RELAXATION = 0.7
AGG1 = 8
AGG2 = 32
F32, BF16 = jnp.float32, jnp.bfloat16
MESH = pl.DeviceIdType.MESH


def high_part(x):
    return x.astype(BF16)


def low_part(x):
    return (x - x.astype(BF16).astype(F32)).astype(BF16)


def split(x):
    return jnp.concatenate([high_part(x), low_part(x)], axis=0)


def joined(y):
    half = y.shape[0] // 2
    return y[:half] + y[half:]


def mm(x, w):
    return joined(jnp.dot(split(x), w, preferred_element_type=F32))


def dot_nt(x, w):
    return lax.dot_general(x, w, (((1,), (1,)), ((), ())), preferred_element_type=F32)


def mm_nt(x, w):
    return joined(dot_nt(split(x), w))


def iota(shape, dim):
    return lax.broadcasted_iota(jnp.int32, shape, dim)


def kernel(
    ng, nm,
    fcols_ref, gcols_ref, ccols_ref,
    rhs, ftiles, fsends, fweights, fgroups,
    gtiles_hbm, gsends, gweights, ggroups, ctiles_hbm,
    sol_out, res_out,
    fhi, flo, ghi, glo, chi, clo,
    fscale, gscale, cscale,
    gtiles, ctiles, fsel, gsel, fagg, gagg, gplain,
    hp_out, hp_in, hp_hi, hp_lo,
    fext, gext, cext,
    fy, gy, cy,
    x0, x1, zed, img,
    fout, fin, gout, gin, gathered, cparts, sums_m, sums_g,
    fs_send, fs_recv, gs_send, gs_recv, ag_send, ag_recv, cg_send, cg_recv,
    sm_send, sm_recv, sg_send, sg_recv, hp_send, hp_recv, load_sem,
):
    grp, mem = lax.axis_index("grp"), lax.axis_index("mem")
    me = grp * nm + mem
    T = ftiles.shape[-1]
    nrhs = rhs.shape[0]
    nb0, nb1, nb2 = ftiles.shape[0], gtiles.shape[0], ctiles.shape[0]
    rows0, rows1, rows2 = nb0 * T, nb1 * T, nb2 * T
    halo0, halo1 = fsends.shape[1], gsends.shape[1]
    h0, h1 = halo0 // T, halo1 // T
    own1 = rows0 // AGG1
    ob1 = own1 // T
    share = rows1 // AGG2
    place = lax.rem(grp * share, T)
    cblock = lax.div(grp * share, T)

    has_lower, has_upper = me > 0, me < ng * nm - 1
    low_id = jnp.maximum(me - 1, 0)
    up_id = jnp.minimum(me + 1, ng * nm - 1)
    lower = (lax.div(low_id, nm), lax.rem(low_id, nm))
    upper = (lax.div(up_id, nm), lax.rem(up_id, nm))
    g_lower, g_upper = grp > 0, grp < ng - 1
    lower_g = (jnp.maximum(grp - 1, 0), mem)
    upper_g = (jnp.minimum(grp + 1, ng - 1), mem)

    loads = [
        pltpu.make_async_copy(gtiles_hbm, gtiles, load_sem.at[0]),
        pltpu.make_async_copy(ctiles_hbm, ctiles, load_sem.at[1]),
    ]
    for load in loads:
        load.start()

    fin[...] = jnp.zeros_like(fin)
    hp_in[...] = jnp.zeros_like(hp_in)
    gin[...] = jnp.zeros_like(gin)

    def fcols(k, b):
        return fcols_ref[k, b]

    def gcols(k, b):
        return gcols_ref[k, b]

    def ccols(k, b):
        return ccols_ref[b, k]

    barrier = pltpu.get_barrier_semaphore()
    for d in range(1, nm):
        pl.semaphore_signal(barrier, inc=1, device_id=(grp, lax.rem(mem + d, nm)), device_id_type=MESH)
    for d in range(1, ng):
        pl.semaphore_signal(barrier, inc=1, device_id=(lax.rem(grp + d, ng), mem), device_id_type=MESH)

    @pl.when(has_lower)
    def _():
        pl.semaphore_signal(barrier, inc=1, device_id=lower, device_id_type=MESH)

    @pl.when(has_upper)
    def _():
        pl.semaphore_signal(barrier, inc=1, device_id=upper, device_id_type=MESH)

    eye = iota((T, T), 0) == iota((T, T), 1)

    def prepare(tiles, cols, hi, lo, scale, count):
        @pl.loop(0, count)
        def _(b):
            diagonal = jnp.zeros((1, T), F32)
            for k in range(3):
                t = tiles[b, k]
                d = jnp.sum(jnp.where(eye, t, 0.0), axis=0, keepdims=True)
                diagonal = diagonal + jnp.where(cols(k, b) == b, 1.0, 0.0) * d
                hi[b, :, k * T : (k + 1) * T] = high_part(t)
                lo[b, :, k * T : (k + 1) * T] = low_part(t)
            scale[:, pl.ds(pl.multiple_of(b * T, T), T)] = RELAXATION / diagonal

    prepare(ftiles, fcols, fhi, flo, fscale, nb0)

    def one_hot_rows(sel, lists, count):
        width = 2 * lists.shape[1]
        row = jnp.concatenate([lists[0:1, :], lists[1:2, :]], axis=1)

        @pl.loop(0, count)
        def _(b):
            at = pl.multiple_of(b * T, T)
            sel[pl.ds(at, T), :] = jnp.where(iota((T, width), 0) + at == row, 1.0, 0.0).astype(BF16)

    one_hot_rows(fsel, fsends, nb0)

    pl.semaphore_wait(
        barrier, nm - 1 + ng - 1 + has_lower.astype(jnp.int32) + has_upper.astype(jnp.int32)
    )

    def halo_pair(out, into, send, recv, h, slot, low_dev, up_dev):
        def copy(side, dev):
            return pltpu.make_async_remote_copy(
                src_ref=out.at[slot, pl.ds(side * h, h)],
                dst_ref=into.at[slot, pl.ds((1 - side) * h, h)],
                send_sem=send.at[slot, side],
                recv_sem=recv.at[slot, 1 - side],
                device_id=dev,
                device_id_type=MESH,
            )

        return copy(0, low_dev), copy(1, up_dev)

    def f_pair(slot):
        return halo_pair(fout, fin, fs_send, fs_recv, h0, slot, lower, upper)

    def g_pair(slot):
        return halo_pair(gout, gin, gs_send, gs_recv, h1, slot, lower_g, upper_g)

    def start(pair, low, up):
        @pl.when(low)
        def _():
            pair[0].start()

        @pl.when(up)
        def _():
            pair[1].start()

    def finish(pair, low, up):
        @pl.when(low)
        def _():
            pair[0].wait_send()
            pair[1].wait_recv()

        @pl.when(up)
        def _():
            pair[1].wait_send()
            pair[0].wait_recv()

    def fine_send(x, slot):
        picked = mm(x, fsel[...])
        for s in range(2 * h0):
            fout[slot, s] = picked[:, s * T : (s + 1) * T]
        start(f_pair(slot), has_lower, has_upper)

    def group_send(x, slot):
        picked = mm(x, gsel[...])
        for s in range(2 * h1):
            gout[slot, s] = picked[:, s * T : (s + 1) * T]
        start(g_pair(slot), g_lower, g_upper)

    def put_own(x, ext, count):
        parts = split(x)
        for b in range(count):
            ext[b] = parts[:, b * T : (b + 1) * T]

    def apply_own(ext, hi, lo, y, count):
        step = 4 if count % 4 == 0 else (2 if count % 2 == 0 else 1)

        @pl.loop(0, count // step)
        def _(i):
            for j in range(step):
                b = i * step + j
                xs = ext[b]
                r = joined(dot_nt(xs, hi[b, :, :T])) + dot_nt(xs[:nrhs], lo[b, :, :T])
                y[:, pl.ds(pl.multiple_of(b * T, T), T)] = r

    def apply_rest(ext, cols, hi, lo, y, count):
        step = 4 if count % 4 == 0 else (2 if count % 2 == 0 else 1)

        @pl.loop(0, count // step)
        def _(i):
            for j in range(step):
                b = i * step + j
                xs = jnp.concatenate([ext[cols(k, b)] for k in (1, 2)], axis=1)
                r = joined(dot_nt(xs, hi[b, :, T:])) + dot_nt(xs[:nrhs], lo[b, :, T:])
                at = pl.ds(pl.multiple_of(b * T, T), T)
                y[:, at] = y[:, at] + r

    def fine_apply(slot):
        apply_own(fext, fhi, flo, fy, nb0)
        finish(f_pair(slot), has_lower, has_upper)
        for s in range(2 * h0):
            fext[nb0 + s] = split(fin[slot, s])
        apply_rest(fext, fcols, fhi, flo, fy, nb0)
        return fy[...]

    def spread_copies(buf, it, mine, size, send, recv, axis):
        n = nm if axis == "mem" else ng
        out = []
        for d in range(1, n):
            dev = (grp, lax.rem(mem + d, nm)) if axis == "mem" else (lax.rem(grp + d, ng), mem)
            ref = buf.at[it, pl.ds(mine * size, size)]
            out.append(
                pltpu.make_async_remote_copy(
                    src_ref=ref, dst_ref=ref,
                    send_sem=send.at[it, d - 1], recv_sem=recv.at[it, d - 1],
                    device_id=dev, device_id_type=MESH,
                )
            )
        return out

    def run(copies):
        for c in copies:
            c.start()
        for c in copies:
            c.wait()

    def reduced(quantities, it):
        lanes = iota((8, T), 1)
        packed = jnp.zeros((8, T), F32)
        groups = nrhs // 8
        nq = len(quantities)
        for q, (a, b) in enumerate(quantities):
            s = jnp.sum(a * b, axis=1, keepdims=True)
            for k in range(groups):
                packed = jnp.where(lanes == k * nq + q, s[8 * k : 8 * k + 8], packed)
        sums_m[it, mem] = packed
        run(spread_copies(sums_m, it, mem, 1, sm_send, sm_recv, "mem"))
        total = sums_m[it, 0]
        for m in range(1, nm):
            total = total + sums_m[it, m]
        sums_g[it, grp] = total
        run(spread_copies(sums_g, it, grp, 1, sg_send, sg_recv, "grp"))
        total = sums_g[it, 0]
        for g in range(1, ng):
            total = total + sums_g[it, g]
        return [
            jnp.concatenate([total[:, k * nq + q : k * nq + q + 1] for k in range(groups)], axis=0)
            for q in range(nq)
        ]

    res_out[...] = rhs[...]
    start_x = fscale[...] * rhs[...]
    fine_send(start_x, 0)
    put_own(start_x, fext, nb0)
    x0[...] = start_x

    fagg[...] = jnp.where(iota((own1, rows0), 0) == fgroups[...], 1.0, 0.0).astype(BF16)
    gagg[...] = jnp.where(iota((T, rows1), 0) == ggroups[...] + place, 1.0, 0.0).astype(BF16)
    gplain[...] = jnp.where(iota((T, rows1), 0) == ggroups[...], 1.0, 0.0).astype(BF16)
    one_hot_rows(gsel, gsends, nb1)

    table = mm(gagg[...].astype(F32) * gweights[...], gsel[...])
    for side in range(2):
        hp_out[0, side] = table[:, side * halo1 : (side + 1) * halo1]

    def hp_copy(side, dev):
        return pltpu.make_async_remote_copy(
            src_ref=hp_out.at[0, side], dst_ref=hp_in.at[0, 1 - side],
            send_sem=hp_send.at[0, side], recv_sem=hp_recv.at[0, 1 - side],
            device_id=dev, device_id_type=MESH,
        )

    hp_pair = (hp_copy(0, lower_g), hp_copy(1, upper_g))
    start(hp_pair, g_lower, g_upper)
    for load in loads:
        load.wait()
    prepare(gtiles, gcols, ghi, glo, gscale, nb1)
    prepare(ctiles, ccols, chi, clo, cscale, nb2)

    per = T // share
    piece = nrhs // per
    lane = iota((piece, T), 1)

    def packed_part(part):
        out = part[:piece]
        for k in range(1, per):
            out = out + pltpu.roll(part[k * piece : (k + 1) * piece], k * share, 1)
        return out

    def coarse_block(it, c):
        rows = []
        for k in range(per):
            total = jnp.zeros((piece, T), F32)
            for r in range(per):
                shift = ((r - k) * share) % T
                got = cparts[it, c * per + r]
                if shift:
                    got = pltpu.roll(got, shift, 1)
                total = jnp.where((lane >= r * share) & (lane < (r + 1) * share), got, total)
            rows.append(total)
        return jnp.concatenate(rows, axis=0)

    for it in range(ITERS):
        base = 3 * it
        left = res_out[...] - (fine_apply(base) if it == 0 else fy[...])
        lowered = mm_nt(left * fweights[...], fagg[...])
        for s in range(ob1):
            gathered[it, mem * ob1 + s] = lowered[:, s * T : (s + 1) * T]
        run(spread_copies(gathered, it, mem, ob1, ag_send, ag_recv, "mem"))
        b1 = jnp.concatenate([gathered[it, b] for b in range(nb1)], axis=1)
        first = gscale[...] * b1
        group_send(first, it)
        put_own(first, gext, nb1)
        apply_own(gext, ghi, glo, gy, nb1)
        finish(g_pair(it), g_lower, g_upper)
        for s in range(2 * h1):
            gext[nb1 + s] = split(gin[it, s])
        apply_rest(gext, gcols, ghi, glo, gy, nb1)
        left = b1 - gy[...]
        cparts[it, grp] = packed_part(mm_nt(left * gweights[...], gplain[...]))
        run(spread_copies(cparts, it, grp, 1, cg_send, cg_recv, "grp"))
        b2 = jnp.concatenate([coarse_block(it, c) for c in range(nb2)], axis=1)
        x2 = cscale[...] * b2
        put_own(x2, cext, nb2)
        apply_own(cext, chi, clo, cy, nb2)
        apply_rest(cext, ccols, chi, clo, cy, nb2)
        cy[...] = x2 + cscale[...] * (b2 - cy[...])
        raised = cy[:, pl.ds(pl.multiple_of(cblock * T, T), T)]
        x1v = first + gweights[...] * mm(raised, gagg[...])
        put_own(x1v, gext, nb1)
        if it == 0:
            finish(hp_pair, g_lower, g_upper)
            for side in range(2):
                hp_hi[side] = high_part(hp_in[0, side])
                hp_lo[side] = low_part(hp_in[0, side])
        for side in range(2):
            other = jnp.clip(grp + 2 * side - 1, 0, ng - 1)
            oblock = lax.div(other * share, T)
            far = split(cy[:, pl.ds(pl.multiple_of(oblock * T, T), T)])
            lift = joined(jnp.dot(far, hp_hi[side], preferred_element_type=F32)) + jnp.dot(
                far[:nrhs], hp_lo[side], preferred_element_type=F32
            )
            for s in range(h1):
                at = side * h1 + s
                gext[nb1 + at] = split(gin[it, at] + lift[:, s * T : (s + 1) * T])
        apply_own(gext, ghi, glo, gy, nb1)
        apply_rest(gext, gcols, ghi, glo, gy, nb1)
        x1[...] = x1v + gscale[...] * (b1 - gy[...])
        mine = x1[:, pl.ds(pl.multiple_of(mem * own1, T), own1)]
        x0v = x0[...] + fweights[...] * mm(mine, fagg[...])
        fine_send(x0v, base + 1)
        put_own(x0v, fext, nb0)
        z = x0v + fscale[...] * (res_out[...] - fine_apply(base + 1))
        fine_send(z, base + 2)
        put_own(z, fext, nb0)
        q = fine_apply(base + 2)
        if it == 0:
            zed[...] = z
            img[...] = q
            fine_send(fscale[...] * q, base + 3)
            energy, curvature = reduced([(res_out[...], z), (z, q)], it)
            step = energy / curvature
            sol_out[...] = step * zed[...]
            res = res_out[...] - step * img[...]
            res_out[...] = res
            x0v = fscale[...] * res
            x0[...] = x0v
            put_own(x0v, fext, nb0)
            finish(f_pair(base + 3), has_lower, has_upper)
            for s in range(2 * h0):
                fext[nb0 + s] = split(fin[0, s] - step * fin[base + 3, s])
            apply_own(fext, fhi, flo, fy, nb0)
            apply_rest(fext, fcols, fhi, flo, fy, nb0)
        else:
            fresh, own, one, two = reduced(
                [(res_out[...], z), (z, q), (z, img[...]), (zed[...], q)], it
            )
            ratio = fresh / energy
            curvature = own + ratio * (one + two) + ratio * ratio * curvature
            step = fresh / curvature
            sol_out[...] = sol_out[...] + step * (z + ratio * zed[...])
            res_out[...] = res_out[...] - step * (q + ratio * img[...])


def shards(
    ng, nm,
    right_side, fine_tiles, fine_columns, fine_sends, fine_weights, fine_groups,
    group_tiles, group_columns, group_sends, group_weights, group_groups,
    coarse_tiles, coarse_columns,
):
    nrhs, rows0 = right_side.shape
    T = fine_tiles.shape[-1]
    nb0, nb1, nb2 = fine_tiles.shape[0], group_tiles.shape[0], coarse_tiles.shape[0]
    rows1, rows2 = nb1 * T, nb2 * T
    h0, h1 = fine_sends.shape[1] // T, group_sends.shape[1] // T
    own1 = rows0 // AGG1
    vm, dma = pltpu.VMEM, pltpu.SemaphoreType.DMA
    scratch = [
        vm((nb0, T, 3 * T), BF16), vm((nb0, T, 3 * T), BF16),
        vm((nb1, T, 3 * T), BF16), vm((nb1, T, 3 * T), BF16),
        vm((nb2, T, 3 * T), BF16), vm((nb2, T, 3 * T), BF16),
        vm((1, rows0), F32), vm((1, rows1), F32), vm((1, rows2), F32),
        vm(group_tiles.shape, F32), vm(coarse_tiles.shape, F32),
        vm((rows0, 2 * h0 * T), BF16), vm((rows1, 2 * h1 * T), BF16),
        vm((own1, rows0), BF16), vm((T, rows1), BF16), vm((T, rows1), BF16),
        vm((1, 2, T, h1 * T), F32), vm((1, 2, T, h1 * T), F32),
        vm((2, T, h1 * T), BF16), vm((2, T, h1 * T), BF16),
        vm((nb0 + 2 * h0, 2 * nrhs, T), BF16),
        vm((nb1 + 2 * h1, 2 * nrhs, T), BF16),
        vm((nb2, 2 * nrhs, T), BF16),
        vm((nrhs, rows0), F32), vm((nrhs, rows1), F32), vm((nrhs, rows2), F32),
        vm((nrhs, rows0), F32), vm((nrhs, rows1), F32),
        vm((nrhs, rows0), F32), vm((nrhs, rows0), F32),
        vm((3 * ITERS, 2 * h0, nrhs, T), F32), vm((3 * ITERS, 2 * h0, nrhs, T), F32),
        vm((ITERS, 2 * h1, nrhs, T), F32), vm((ITERS, 2 * h1, nrhs, T), F32),
        vm((ITERS, nb1, nrhs, T), F32), vm((ITERS, ng, nrhs * (rows1 // AGG2) // T, T), F32),
        vm((ITERS, nm, 8, T), F32), vm((ITERS, ng, 8, T), F32),
        dma((3 * ITERS, 2)), dma((3 * ITERS, 2)),
        dma((ITERS, 2)), dma((ITERS, 2)),
        dma((ITERS, nm - 1)), dma((ITERS, nm - 1)),
        dma((ITERS, ng - 1)), dma((ITERS, ng - 1)),
        dma((ITERS, nm - 1)), dma((ITERS, nm - 1)),
        dma((ITERS, ng - 1)), dma((ITERS, ng - 1)),
        dma((1, 2)), dma((1, 2)), dma((2,)),
    ]
    in_vm, in_sm = pl.BlockSpec(memory_space=pltpu.VMEM), pl.BlockSpec(memory_space=pltpu.SMEM)
    in_any = pl.BlockSpec(memory_space=pl.ANY)
    out = jax.ShapeDtypeStruct((nrhs, rows0), F32)
    return pl.pallas_call(
        functools.partial(kernel, ng, nm),
        out_shape=(out, out),
        in_specs=[in_sm] * 3 + [in_vm] * 5 + [in_any] + [in_vm] * 3 + [in_any],
        out_specs=(in_vm, in_vm),
        scratch_shapes=scratch,
        compiler_params=pltpu.CompilerParams(
            collective_id=0, has_side_effects=True, vmem_limit_bytes=60 << 20
        ),
    )(
        fine_columns.T, group_columns.T, coarse_columns,
        right_side, fine_tiles, fine_sends, fine_weights.reshape(1, -1),
        fine_groups.reshape(1, -1), group_tiles, group_sends,
        group_weights.reshape(1, -1), group_groups.reshape(1, -1), coarse_tiles,
    )


def solution(mesh):
    both = ("grp", "mem")
    return jax.shard_map(
        functools.partial(shards, mesh.shape["grp"], mesh.shape["mem"]),
        mesh=mesh,
        in_specs=(
            P(None, both), P(both, None, None, None), P(both, None), P(both, None), P(both), P(both),
            P("grp", None, None, None), P("grp", None), P("grp", None), P("grp"), P("grp"),
            P(), P(),
        ),
        out_specs=(P(None, both), P(None, both)),
        check_vma=False,
    )
```

```python
import functools

import jax
import jax.numpy as jnp
from jax import lax
from jax.experimental import pallas as pl
from jax.experimental.pallas import tpu as pltpu
from jax.sharding import PartitionSpec as P

ITERS = 2
RELAXATION = 0.7
AGG1 = 8
AGG2 = 32
F32, BF16 = jnp.float32, jnp.bfloat16
MESH = pl.DeviceIdType.MESH


def high_part(x):
    return x.astype(BF16)


def low_part(x):
    return (x - x.astype(BF16).astype(F32)).astype(BF16)


def split(x):
    return jnp.concatenate([high_part(x), low_part(x)], axis=0)


def joined(y):
    half = y.shape[0] // 2
    return y[:half] + y[half:]


def mm(x, w):
    return joined(jnp.dot(split(x), w, preferred_element_type=F32))


def dot_nt(x, w):
    return lax.dot_general(x, w, (((1,), (1,)), ((), ())), preferred_element_type=F32)


def mm_nt(x, w):
    return joined(dot_nt(split(x), w))


def iota(shape, dim):
    return lax.broadcasted_iota(jnp.int32, shape, dim)


def kernel(
    ng, nm,
    fcols_ref, gcols_ref, ccols_ref,
    rhs, ftiles, fsends, fweights, fgroups,
    gtiles_hbm, gsends, gweights, ggroups, ctiles_hbm,
    sol_out, res_out,
    fhi, flo, ghi, glo, chi, clo,
    fscale, gscale, cscale,
    gtiles, ctiles, fsel, gsel, fagg, gagg, gplain,
    hp_out, hp_in, hp_hi, hp_lo,
    fext, gext, cext,
    fy, gy, cy,
    x0, x1, zed, img,
    fout, fin, gout, gin, gathered, cparts, sums_m, sums_g,
    fs_send, fs_recv, gs_send, gs_recv, ag_send, ag_recv, cg_send, cg_recv,
    sm_send, sm_recv, sg_send, sg_recv, hp_send, hp_recv, load_sem,
):
    grp, mem = lax.axis_index("grp"), lax.axis_index("mem")
    me = grp * nm + mem
    T = ftiles.shape[-1]
    nrhs = rhs.shape[0]
    nb0, nb1, nb2 = ftiles.shape[0], gtiles.shape[0], ctiles.shape[0]
    rows0, rows1, rows2 = nb0 * T, nb1 * T, nb2 * T
    halo0, halo1 = fsends.shape[1], gsends.shape[1]
    h0, h1 = halo0 // T, halo1 // T
    own1 = rows0 // AGG1
    ob1 = own1 // T
    share = rows1 // AGG2
    place = lax.rem(grp * share, T)
    cblock = lax.div(grp * share, T)

    has_lower, has_upper = me > 0, me < ng * nm - 1
    low_id = jnp.maximum(me - 1, 0)
    up_id = jnp.minimum(me + 1, ng * nm - 1)
    lower = (lax.div(low_id, nm), lax.rem(low_id, nm))
    upper = (lax.div(up_id, nm), lax.rem(up_id, nm))
    g_lower, g_upper = grp > 0, grp < ng - 1
    lower_g = (jnp.maximum(grp - 1, 0), mem)
    upper_g = (jnp.minimum(grp + 1, ng - 1), mem)

    loads = [
        pltpu.make_async_copy(gtiles_hbm, gtiles, load_sem.at[0]),
        pltpu.make_async_copy(ctiles_hbm, ctiles, load_sem.at[1]),
    ]
    for load in loads:
        load.start()

    fin[...] = jnp.zeros_like(fin)
    hp_in[...] = jnp.zeros_like(hp_in)
    gin[...] = jnp.zeros_like(gin)

    def fcols(k, b):
        return fcols_ref[k, b]

    def gcols(k, b):
        return gcols_ref[k, b]

    def ccols(k, b):
        return ccols_ref[b, k]

    barrier = pltpu.get_barrier_semaphore()
    for d in range(1, nm):
        pl.semaphore_signal(barrier, inc=1, device_id=(grp, lax.rem(mem + d, nm)), device_id_type=MESH)
    for d in range(1, ng):
        pl.semaphore_signal(barrier, inc=1, device_id=(lax.rem(grp + d, ng), mem), device_id_type=MESH)

    @pl.when(has_lower)
    def _():
        pl.semaphore_signal(barrier, inc=1, device_id=lower, device_id_type=MESH)

    @pl.when(has_upper)
    def _():
        pl.semaphore_signal(barrier, inc=1, device_id=upper, device_id_type=MESH)

    eye = iota((T, T), 0) == iota((T, T), 1)

    def prepare(tiles, cols, hi, lo, scale, count):
        @pl.loop(0, count)
        def _(b):
            diagonal = jnp.zeros((1, T), F32)
            for k in range(3):
                t = tiles[b, k]
                d = jnp.sum(jnp.where(eye, t, 0.0), axis=0, keepdims=True)
                diagonal = diagonal + jnp.where(cols(k, b) == b, 1.0, 0.0) * d
                hi[b, :, k * T : (k + 1) * T] = high_part(t)
                lo[b, :, k * T : (k + 1) * T] = low_part(t)
            scale[:, pl.ds(pl.multiple_of(b * T, T), T)] = RELAXATION / diagonal

    prepare(ftiles, fcols, fhi, flo, fscale, nb0)

    def one_hot_rows(sel, lists, count):
        width = 2 * lists.shape[1]
        row = jnp.concatenate([lists[0:1, :], lists[1:2, :]], axis=1)

        @pl.loop(0, count)
        def _(b):
            at = pl.multiple_of(b * T, T)
            sel[pl.ds(at, T), :] = jnp.where(iota((T, width), 0) + at == row, 1.0, 0.0).astype(BF16)

    one_hot_rows(fsel, fsends, nb0)

    pl.semaphore_wait(
        barrier, nm - 1 + ng - 1 + has_lower.astype(jnp.int32) + has_upper.astype(jnp.int32)
    )

    def halo_pair(out, into, send, recv, h, slot, low_dev, up_dev):
        def copy(side, dev):
            return pltpu.make_async_remote_copy(
                src_ref=out.at[slot, pl.ds(side * h, h)],
                dst_ref=into.at[slot, pl.ds((1 - side) * h, h)],
                send_sem=send.at[slot, side],
                recv_sem=recv.at[slot, 1 - side],
                device_id=dev,
                device_id_type=MESH,
            )

        return copy(0, low_dev), copy(1, up_dev)

    def f_pair(slot):
        return halo_pair(fout, fin, fs_send, fs_recv, h0, slot, lower, upper)

    def g_pair(slot):
        return halo_pair(gout, gin, gs_send, gs_recv, h1, slot, lower_g, upper_g)

    def start(pair, low, up):
        @pl.when(low)
        def _():
            pair[0].start()

        @pl.when(up)
        def _():
            pair[1].start()

    def finish(pair, low, up):
        @pl.when(low)
        def _():
            pair[0].wait_send()
            pair[1].wait_recv()

        @pl.when(up)
        def _():
            pair[1].wait_send()
            pair[0].wait_recv()

    def fine_send(x, slot):
        picked = mm(x, fsel[...])
        for s in range(2 * h0):
            fout[slot, s] = picked[:, s * T : (s + 1) * T]
        start(f_pair(slot), has_lower, has_upper)

    def group_send(x, slot):
        picked = mm(x, gsel[...])
        for s in range(2 * h1):
            gout[slot, s] = picked[:, s * T : (s + 1) * T]
        start(g_pair(slot), g_lower, g_upper)
        return picked

    def put_own(x, ext, count):
        parts = split(x)
        for b in range(count):
            ext[b] = parts[:, b * T : (b + 1) * T]

    def apply_own(ext, hi, lo, y, count):
        step = 4 if count % 4 == 0 else (2 if count % 2 == 0 else 1)

        @pl.loop(0, count // step)
        def _(i):
            for j in range(step):
                b = i * step + j
                xs = ext[b]
                r = joined(dot_nt(xs, hi[b, :, :T])) + dot_nt(xs[:nrhs], lo[b, :, :T])
                y[:, pl.ds(pl.multiple_of(b * T, T), T)] = r

    def apply_rest(ext, cols, hi, lo, y, count):
        step = 4 if count % 4 == 0 else (2 if count % 2 == 0 else 1)

        @pl.loop(0, count // step)
        def _(i):
            for j in range(step):
                b = i * step + j
                xs = jnp.concatenate([ext[cols(k, b)] for k in (1, 2)], axis=1)
                r = joined(dot_nt(xs, hi[b, :, T:])) + dot_nt(xs[:nrhs], lo[b, :, T:])
                at = pl.ds(pl.multiple_of(b * T, T), T)
                y[:, at] = y[:, at] + r

    def fine_apply(slot):
        apply_own(fext, fhi, flo, fy, nb0)
        finish(f_pair(slot), has_lower, has_upper)
        for s in range(2 * h0):
            fext[nb0 + s] = split(fin[slot, s])
        apply_rest(fext, fcols, fhi, flo, fy, nb0)
        return fy[...]

    def spread_copies(buf, it, mine, size, send, recv, axis):
        n = nm if axis == "mem" else ng
        out = []
        for d in range(1, n):
            dev = (grp, lax.rem(mem + d, nm)) if axis == "mem" else (lax.rem(grp + d, ng), mem)
            ref = buf.at[it, pl.ds(mine * size, size)]
            out.append(
                pltpu.make_async_remote_copy(
                    src_ref=ref, dst_ref=ref,
                    send_sem=send.at[it, d - 1], recv_sem=recv.at[it, d - 1],
                    device_id=dev, device_id_type=MESH,
                )
            )
        return out

    def run(copies):
        for c in copies:
            c.start()
        for c in copies:
            c.wait()

    def reduced(quantities, it):
        lanes = iota((8, T), 1)
        packed = jnp.zeros((8, T), F32)
        groups = nrhs // 8
        nq = len(quantities)
        for q, (a, b) in enumerate(quantities):
            s = jnp.sum(a * b, axis=1, keepdims=True)
            for k in range(groups):
                packed = jnp.where(lanes == k * nq + q, s[8 * k : 8 * k + 8], packed)
        sums_m[it, mem] = packed
        run(spread_copies(sums_m, it, mem, 1, sm_send, sm_recv, "mem"))
        total = sums_m[it, 0]
        for m in range(1, nm):
            total = total + sums_m[it, m]
        sums_g[it, grp] = total
        run(spread_copies(sums_g, it, grp, 1, sg_send, sg_recv, "grp"))
        total = sums_g[it, 0]
        for g in range(1, ng):
            total = total + sums_g[it, g]
        return [
            jnp.concatenate([total[:, k * nq + q : k * nq + q + 1] for k in range(groups)], axis=0)
            for q in range(nq)
        ]

    res_out[...] = rhs[...]
    start_x = fscale[...] * rhs[...]
    fine_send(start_x, 0)
    put_own(start_x, fext, nb0)
    x0[...] = start_x

    fagg[...] = jnp.where(iota((own1, rows0), 0) == fgroups[...], 1.0, 0.0).astype(BF16)
    gagg[...] = jnp.where(iota((T, rows1), 0) == ggroups[...] + place, 1.0, 0.0).astype(BF16)
    gplain[...] = jnp.where(iota((T, rows1), 0) == ggroups[...], 1.0, 0.0).astype(BF16)
    one_hot_rows(gsel, gsends, nb1)

    table = mm(gagg[...].astype(F32) * gweights[...], gsel[...])
    for side in range(2):
        hp_out[side, 0] = table[:, side * halo1 : (side + 1) * halo1]
        hp_out[side, 1] = jnp.zeros((T, halo1), F32)
    for load in loads:
        load.wait()
    prepare(gtiles, gcols, ghi, glo, gscale, nb1)

    @pl.loop(0, nb1)
    def _(b):
        at = pl.ds(pl.multiple_of(b * T, T), T)
        w = split(gplain[:share, at].astype(F32) * gweights[:, at])
        r = joined(jnp.dot(w, ghi[b, :, T:], preferred_element_type=F32)) + jnp.dot(
            w[:share], glo[b, :, T:], preferred_element_type=F32
        )
        for k in (1, 2):
            for i in range(2 * h1):
                side, s = i // h1, i % h1
                hit = jnp.where(gcols(k, b) == nb1 + i, 1.0, 0.0)
                span = slice(s * T, (s + 1) * T)
                hp_out[side, 1, :share, span] = (
                    hp_out[side, 1, :share, span] + hit * r[:, (k - 1) * T : k * T]
                )

    def hp_copy(side, dev):
        return pltpu.make_async_remote_copy(
            src_ref=hp_out.at[side], dst_ref=hp_in.at[1 - side],
            send_sem=hp_send.at[0, side], recv_sem=hp_recv.at[0, 1 - side],
            device_id=dev, device_id_type=MESH,
        )

    hp_pair = (hp_copy(0, lower_g), hp_copy(1, upper_g))
    start(hp_pair, g_lower, g_upper)
    prepare(ctiles, ccols, chi, clo, cscale, nb2)

    per = T // share
    piece = nrhs // per
    lane = iota((piece, T), 1)

    def packed_part(part):
        out = part[:piece]
        for k in range(1, per):
            out = out + pltpu.roll(part[k * piece : (k + 1) * piece], k * share, 1)
        return out

    def coarse_block(it, c):
        rows = []
        for k in range(per):
            total = jnp.zeros((piece, T), F32)
            for r in range(per):
                shift = ((r - k) * share) % T
                g = c * per + r
                got = cparts[it, g, :piece]
                if g > 0:
                    got = got + cparts[it, g - 1, 2 * piece :]
                if g < ng - 1:
                    got = got + cparts[it, g + 1, piece : 2 * piece]
                if shift:
                    got = pltpu.roll(got, shift, 1)
                total = jnp.where((lane >= r * share) & (lane < (r + 1) * share), got, total)
            rows.append(total)
        return jnp.concatenate(rows, axis=0)

    for it in range(ITERS):
        base = 3 * it
        left = res_out[...] - (fine_apply(base) if it == 0 else fy[...])
        lowered = mm_nt(left * fweights[...], fagg[...])
        for s in range(ob1):
            gathered[it, mem * ob1 + s] = lowered[:, s * T : (s + 1) * T]
        run(spread_copies(gathered, it, mem, ob1, ag_send, ag_recv, "mem"))
        b1 = jnp.concatenate([gathered[it, b] for b in range(nb1)], axis=1)
        first = gscale[...] * b1
        picked = group_send(first, it)
        put_own(first, gext, nb1)
        for s in range(2 * h1):
            gext[nb1 + s] = jnp.zeros((2 * nrhs, T), BF16)
        apply_own(gext, ghi, glo, gy, nb1)
        apply_rest(gext, gcols, ghi, glo, gy, nb1)
        left = b1 - gy[...]
        cparts[it, grp, :piece] = packed_part(mm_nt(left * gweights[...], gplain[...]))
        if it == 0:
            finish(hp_pair, g_lower, g_upper)
            for side in range(2):
                for which in range(2):
                    hp_hi[side, which] = high_part(hp_in[side, which])
                    hp_lo[side, which] = low_part(hp_in[side, which])
        for side in range(2):
            given = split(picked[:, side * halo1 : (side + 1) * halo1])
            felt = joined(dot_nt(given, hp_hi[side, 1])) + dot_nt(given[:nrhs], hp_lo[side, 1])
            cparts[it, grp, (side + 1) * piece : (side + 2) * piece] = packed_part(-felt)
        run(spread_copies(cparts, it, grp, 1, cg_send, cg_recv, "grp"))
        b2 = jnp.concatenate([coarse_block(it, c) for c in range(nb2)], axis=1)
        x2 = cscale[...] * b2
        put_own(x2, cext, nb2)
        apply_own(cext, chi, clo, cy, nb2)
        apply_rest(cext, ccols, chi, clo, cy, nb2)
        cy[...] = x2 + cscale[...] * (b2 - cy[...])
        raised = cy[:, pl.ds(pl.multiple_of(cblock * T, T), T)]
        x1v = first + gweights[...] * mm(raised, gagg[...])
        put_own(x1v, gext, nb1)
        finish(g_pair(it), g_lower, g_upper)
        for side in range(2):
            other = jnp.clip(grp + 2 * side - 1, 0, ng - 1)
            oblock = lax.div(other * share, T)
            far = split(cy[:, pl.ds(pl.multiple_of(oblock * T, T), T)])
            lift = joined(jnp.dot(far, hp_hi[side, 0], preferred_element_type=F32)) + jnp.dot(
                far[:nrhs], hp_lo[side, 0], preferred_element_type=F32
            )
            for s in range(h1):
                at = side * h1 + s
                gext[nb1 + at] = split(gin[it, at] + lift[:, s * T : (s + 1) * T])
        apply_own(gext, ghi, glo, gy, nb1)
        apply_rest(gext, gcols, ghi, glo, gy, nb1)
        x1[...] = x1v + gscale[...] * (b1 - gy[...])
        mine = x1[:, pl.ds(pl.multiple_of(mem * own1, T), own1)]
        x0v = x0[...] + fweights[...] * mm(mine, fagg[...])
        fine_send(x0v, base + 1)
        put_own(x0v, fext, nb0)
        z = x0v + fscale[...] * (res_out[...] - fine_apply(base + 1))
        fine_send(z, base + 2)
        put_own(z, fext, nb0)
        q = fine_apply(base + 2)
        if it == 0:
            zed[...] = z
            img[...] = q
            fine_send(fscale[...] * q, base + 3)
            energy, curvature = reduced([(res_out[...], z), (z, q)], it)
            step = energy / curvature
            sol_out[...] = step * zed[...]
            res = res_out[...] - step * img[...]
            res_out[...] = res
            x0v = fscale[...] * res
            x0[...] = x0v
            put_own(x0v, fext, nb0)
            finish(f_pair(base + 3), has_lower, has_upper)
            for s in range(2 * h0):
                fext[nb0 + s] = split(fin[0, s] - step * fin[base + 3, s])
            apply_own(fext, fhi, flo, fy, nb0)
            apply_rest(fext, fcols, fhi, flo, fy, nb0)
        else:
            fresh, own, one, two = reduced(
                [(res_out[...], z), (z, q), (z, img[...]), (zed[...], q)], it
            )
            ratio = fresh / energy
            curvature = own + ratio * (one + two) + ratio * ratio * curvature
            step = fresh / curvature
            sol_out[...] = sol_out[...] + step * (z + ratio * zed[...])
            res_out[...] = res_out[...] - step * (q + ratio * img[...])


def shards(
    ng, nm,
    right_side, fine_tiles, fine_columns, fine_sends, fine_weights, fine_groups,
    group_tiles, group_columns, group_sends, group_weights, group_groups,
    coarse_tiles, coarse_columns,
):
    nrhs, rows0 = right_side.shape
    T = fine_tiles.shape[-1]
    nb0, nb1, nb2 = fine_tiles.shape[0], group_tiles.shape[0], coarse_tiles.shape[0]
    rows1, rows2 = nb1 * T, nb2 * T
    h0, h1 = fine_sends.shape[1] // T, group_sends.shape[1] // T
    own1 = rows0 // AGG1
    vm, dma = pltpu.VMEM, pltpu.SemaphoreType.DMA
    scratch = [
        vm((nb0, T, 3 * T), BF16), vm((nb0, T, 3 * T), BF16),
        vm((nb1, T, 3 * T), BF16), vm((nb1, T, 3 * T), BF16),
        vm((nb2, T, 3 * T), BF16), vm((nb2, T, 3 * T), BF16),
        vm((1, rows0), F32), vm((1, rows1), F32), vm((1, rows2), F32),
        vm(group_tiles.shape, F32), vm(coarse_tiles.shape, F32),
        vm((rows0, 2 * h0 * T), BF16), vm((rows1, 2 * h1 * T), BF16),
        vm((own1, rows0), BF16), vm((T, rows1), BF16), vm((T, rows1), BF16),
        vm((2, 2, T, h1 * T), F32), vm((2, 2, T, h1 * T), F32),
        vm((2, 2, T, h1 * T), BF16), vm((2, 2, T, h1 * T), BF16),
        vm((nb0 + 2 * h0, 2 * nrhs, T), BF16),
        vm((nb1 + 2 * h1, 2 * nrhs, T), BF16),
        vm((nb2, 2 * nrhs, T), BF16),
        vm((nrhs, rows0), F32), vm((nrhs, rows1), F32), vm((nrhs, rows2), F32),
        vm((nrhs, rows0), F32), vm((nrhs, rows1), F32),
        vm((nrhs, rows0), F32), vm((nrhs, rows0), F32),
        vm((3 * ITERS, 2 * h0, nrhs, T), F32), vm((3 * ITERS, 2 * h0, nrhs, T), F32),
        vm((ITERS, 2 * h1, nrhs, T), F32), vm((ITERS, 2 * h1, nrhs, T), F32),
        vm((ITERS, nb1, nrhs, T), F32), vm((ITERS, ng, 3 * nrhs * (rows1 // AGG2) // T, T), F32),
        vm((ITERS, nm, 8, T), F32), vm((ITERS, ng, 8, T), F32),
        dma((3 * ITERS, 2)), dma((3 * ITERS, 2)),
        dma((ITERS, 2)), dma((ITERS, 2)),
        dma((ITERS, nm - 1)), dma((ITERS, nm - 1)),
        dma((ITERS, ng - 1)), dma((ITERS, ng - 1)),
        dma((ITERS, nm - 1)), dma((ITERS, nm - 1)),
        dma((ITERS, ng - 1)), dma((ITERS, ng - 1)),
        dma((1, 2)), dma((1, 2)), dma((2,)),
    ]
    in_vm, in_sm = pl.BlockSpec(memory_space=pltpu.VMEM), pl.BlockSpec(memory_space=pltpu.SMEM)
    in_any = pl.BlockSpec(memory_space=pl.ANY)
    out = jax.ShapeDtypeStruct((nrhs, rows0), F32)
    return pl.pallas_call(
        functools.partial(kernel, ng, nm),
        out_shape=(out, out),
        in_specs=[in_sm] * 3 + [in_vm] * 5 + [in_any] + [in_vm] * 3 + [in_any],
        out_specs=(in_vm, in_vm),
        scratch_shapes=scratch,
        compiler_params=pltpu.CompilerParams(
            collective_id=0, has_side_effects=True, vmem_limit_bytes=60 << 20
        ),
    )(
        fine_columns.T, group_columns.T, coarse_columns,
        right_side, fine_tiles, fine_sends, fine_weights.reshape(1, -1),
        fine_groups.reshape(1, -1), group_tiles, group_sends,
        group_weights.reshape(1, -1), group_groups.reshape(1, -1), coarse_tiles,
    )


def solution(mesh):
    both = ("grp", "mem")
    return jax.shard_map(
        functools.partial(shards, mesh.shape["grp"], mesh.shape["mem"]),
        mesh=mesh,
        in_specs=(
            P(None, both), P(both, None, None, None), P(both, None), P(both, None), P(both), P(both),
            P("grp", None, None, None), P("grp", None), P("grp", None), P("grp"), P("grp"),
            P(), P(),
        ),
        out_specs=(P(None, both), P(None, both)),
        check_vma=False,
    )
```

```python
import functools

import jax
import jax.numpy as jnp
from jax import lax
from jax.experimental import pallas as pl
from jax.experimental.pallas import tpu as pltpu
from jax.sharding import PartitionSpec as P

ITERS = 2
RELAXATION = 0.7
AGG1 = 8
AGG2 = 32
F32, BF16 = jnp.float32, jnp.bfloat16
MESH = pl.DeviceIdType.MESH


def high_part(x):
    return x.astype(BF16)


def low_part(x):
    return (x - x.astype(BF16).astype(F32)).astype(BF16)


def split(x):
    return jnp.concatenate([high_part(x), low_part(x)], axis=0)


def joined(y):
    half = y.shape[0] // 2
    return y[:half] + y[half:]


def mm(x, w):
    return joined(jnp.dot(split(x), w, preferred_element_type=F32))


def dot_nt(x, w):
    return lax.dot_general(x, w, (((1,), (1,)), ((), ())), preferred_element_type=F32)


def mm_nt(x, w):
    return joined(dot_nt(split(x), w))


def iota(shape, dim):
    return lax.broadcasted_iota(jnp.int32, shape, dim)


def kernel(
    ng, nm,
    fcols_ref, gcols_ref, ccols_ref,
    rhs, ftiles, fsends, fweights, fgroups,
    gtiles_hbm, gsends, gweights, ggroups, ctiles_hbm,
    both_out,
    fhi, flo, ghi, glo, chi, clo,
    fscale, gscale, cscale,
    gtiles, ctiles, fsel, gsel, fagg, gagg, gplain,
    hp_out, hp_in, hp_hi, hp_lo,
    fext, gext, cext,
    fy, gy, cy,
    x0, x1, zed, img,
    fout, fin, gout, gin, gathered, cparts, sums_m, sums_g,
    fs_send, fs_recv, gs_send, gs_recv, ag_send, ag_recv, cg_send, cg_recv,
    sm_send, sm_recv, sg_send, sg_recv, hp_send, hp_recv, load_sem,
):
    sol_out, res_out = both_out.at[0], both_out.at[1]
    grp, mem = lax.axis_index("grp"), lax.axis_index("mem")
    me = grp * nm + mem
    T = ftiles.shape[-1]
    nrhs = rhs.shape[0]
    nb0, nb1, nb2 = ftiles.shape[0], gtiles.shape[0], ctiles.shape[0]
    rows0, rows1, rows2 = nb0 * T, nb1 * T, nb2 * T
    halo0, halo1 = fsends.shape[1], gsends.shape[1]
    h0, h1 = halo0 // T, halo1 // T
    own1 = rows0 // AGG1
    ob1 = own1 // T
    share = rows1 // AGG2
    place = lax.rem(grp * share, T)
    cblock = lax.div(grp * share, T)

    has_lower, has_upper = me > 0, me < ng * nm - 1
    low_id = jnp.maximum(me - 1, 0)
    up_id = jnp.minimum(me + 1, ng * nm - 1)
    lower = (lax.div(low_id, nm), lax.rem(low_id, nm))
    upper = (lax.div(up_id, nm), lax.rem(up_id, nm))
    g_lower, g_upper = grp > 0, grp < ng - 1
    lower_g = (jnp.maximum(grp - 1, 0), mem)
    upper_g = (jnp.minimum(grp + 1, ng - 1), mem)

    loads = [
        pltpu.make_async_copy(gtiles_hbm, gtiles, load_sem.at[0]),
        pltpu.make_async_copy(ctiles_hbm, ctiles, load_sem.at[1]),
    ]
    for load in loads:
        load.start()

    fin[...] = jnp.zeros_like(fin)
    hp_in[...] = jnp.zeros_like(hp_in)
    gin[...] = jnp.zeros_like(gin)

    def fcols(k, b):
        return fcols_ref[k, b]

    def gcols(k, b):
        return gcols_ref[k, b]

    def ccols(k, b):
        return ccols_ref[b, k]

    barrier = pltpu.get_barrier_semaphore()
    for d in range(1, nm):
        pl.semaphore_signal(barrier, inc=1, device_id=(grp, lax.rem(mem + d, nm)), device_id_type=MESH)
    for d in range(1, ng):
        pl.semaphore_signal(barrier, inc=1, device_id=(lax.rem(grp + d, ng), mem), device_id_type=MESH)

    @pl.when(has_lower)
    def _():
        pl.semaphore_signal(barrier, inc=1, device_id=lower, device_id_type=MESH)

    @pl.when(has_upper)
    def _():
        pl.semaphore_signal(barrier, inc=1, device_id=upper, device_id_type=MESH)

    eye = iota((T, T), 0) == iota((T, T), 1)

    def prepare(tiles, cols, hi, lo, scale, count):
        @pl.loop(0, count)
        def _(b):
            diagonal = jnp.zeros((1, T), F32)
            for k in range(3):
                t = tiles[b, k]
                d = jnp.sum(jnp.where(eye, t, 0.0), axis=0, keepdims=True)
                diagonal = diagonal + jnp.where(cols(k, b) == b, 1.0, 0.0) * d
                hi[b, :, k * T : (k + 1) * T] = high_part(t)
                lo[b, :, k * T : (k + 1) * T] = low_part(t)
            scale[:, pl.ds(pl.multiple_of(b * T, T), T)] = RELAXATION / diagonal

    prepare(ftiles, fcols, fhi, flo, fscale, nb0)

    def one_hot_rows(sel, lists, count):
        width = 2 * lists.shape[1]
        row = jnp.concatenate([lists[0:1, :], lists[1:2, :]], axis=1)

        @pl.loop(0, count)
        def _(b):
            at = pl.multiple_of(b * T, T)
            sel[pl.ds(at, T), :] = jnp.where(iota((T, width), 0) + at == row, 1.0, 0.0).astype(BF16)

    one_hot_rows(fsel, fsends, nb0)

    pl.semaphore_wait(
        barrier, nm - 1 + ng - 1 + has_lower.astype(jnp.int32) + has_upper.astype(jnp.int32)
    )

    def halo_pair(out, into, send, recv, h, slot, low_dev, up_dev):
        def copy(side, dev):
            return pltpu.make_async_remote_copy(
                src_ref=out.at[slot, pl.ds(side * h, h)],
                dst_ref=into.at[slot, pl.ds((1 - side) * h, h)],
                send_sem=send.at[slot, side],
                recv_sem=recv.at[slot, 1 - side],
                device_id=dev,
                device_id_type=MESH,
            )

        return copy(0, low_dev), copy(1, up_dev)

    def f_pair(slot):
        return halo_pair(fout, fin, fs_send, fs_recv, h0, slot, lower, upper)

    def g_pair(slot):
        return halo_pair(gout, gin, gs_send, gs_recv, h1, slot, lower_g, upper_g)

    def start(pair, low, up):
        @pl.when(low)
        def _():
            pair[0].start()

        @pl.when(up)
        def _():
            pair[1].start()

    def finish(pair, low, up):
        @pl.when(low)
        def _():
            pair[0].wait_send()
            pair[1].wait_recv()

        @pl.when(up)
        def _():
            pair[1].wait_send()
            pair[0].wait_recv()

    def fine_send(x, slot):
        picked = mm(x, fsel[...])
        for s in range(2 * h0):
            fout[slot, s] = picked[:, s * T : (s + 1) * T]
        start(f_pair(slot), has_lower, has_upper)

    def group_send(x, slot):
        picked = mm(x, gsel[...])
        for s in range(2 * h1):
            gout[slot, s] = picked[:, s * T : (s + 1) * T]
        start(g_pair(slot), g_lower, g_upper)
        return picked

    def put_own(x, ext, count):
        parts = split(x)
        for b in range(count):
            ext[b] = parts[:, b * T : (b + 1) * T]

    def apply_own(ext, hi, lo, y, count):
        step = next(n for n in (8, 4, 2, 1) if count % n == 0)

        @pl.loop(0, count // step)
        def _(i):
            for j in range(step):
                b = i * step + j
                xs = ext[b]
                r = joined(dot_nt(xs, hi[b, :, :T])) + dot_nt(xs[:nrhs], lo[b, :, :T])
                y[:, pl.ds(pl.multiple_of(b * T, T), T)] = r

    def apply_rest(ext, cols, hi, lo, y, count):
        step = next(n for n in (8, 4, 2, 1) if count % n == 0)

        @pl.loop(0, count // step)
        def _(i):
            for j in range(step):
                b = i * step + j
                xs = jnp.concatenate([ext[cols(k, b)] for k in (1, 2)], axis=1)
                r = joined(dot_nt(xs, hi[b, :, T:])) + dot_nt(xs[:nrhs], lo[b, :, T:])
                at = pl.ds(pl.multiple_of(b * T, T), T)
                y[:, at] = y[:, at] + r

    def fine_apply(slot):
        apply_own(fext, fhi, flo, fy, nb0)
        finish(f_pair(slot), has_lower, has_upper)
        for s in range(2 * h0):
            fext[nb0 + s] = split(fin[slot, s])
        apply_rest(fext, fcols, fhi, flo, fy, nb0)
        return fy[...]

    def spread_copies(buf, it, mine, size, send, recv, axis):
        n = nm if axis == "mem" else ng
        out = []
        for d in range(1, n):
            dev = (grp, lax.rem(mem + d, nm)) if axis == "mem" else (lax.rem(grp + d, ng), mem)
            ref = buf.at[it, pl.ds(mine * size, size)]
            out.append(
                pltpu.make_async_remote_copy(
                    src_ref=ref, dst_ref=ref,
                    send_sem=send.at[it, d - 1], recv_sem=recv.at[it, d - 1],
                    device_id=dev, device_id_type=MESH,
                )
            )
        return out

    def run(copies):
        for c in copies:
            c.start()
        for c in copies:
            c.wait()

    def reduced(quantities, it, beside=None):
        lanes = iota((8, T), 1)
        packed = jnp.zeros((8, T), F32)
        groups = nrhs // 8
        nq = len(quantities)
        for q, (a, b) in enumerate(quantities):
            s = jnp.sum(a * b, axis=1, keepdims=True)
            for k in range(groups):
                packed = jnp.where(lanes == k * nq + q, s[8 * k : 8 * k + 8], packed)
        sums_m[it, mem] = packed
        copies = spread_copies(sums_m, it, mem, 1, sm_send, sm_recv, "mem")
        for c in copies:
            c.start()
        if beside is not None:
            beside()
        for c in copies:
            c.wait()
        total = sums_m[it, 0]
        for m in range(1, nm):
            total = total + sums_m[it, m]
        sums_g[it, grp] = total
        run(spread_copies(sums_g, it, grp, 1, sg_send, sg_recv, "grp"))
        total = sums_g[it, 0]
        for g in range(1, ng):
            total = total + sums_g[it, g]
        return [
            jnp.concatenate([total[:, k * nq + q : k * nq + q + 1] for k in range(groups)], axis=0)
            for q in range(nq)
        ]

    res_out[...] = rhs[...]
    start_x = fscale[...] * rhs[...]
    fine_send(start_x, 0)
    put_own(start_x, fext, nb0)
    x0[...] = start_x

    fagg[...] = jnp.where(iota((own1, rows0), 0) == fgroups[...], 1.0, 0.0).astype(BF16)
    gagg[...] = jnp.where(iota((T, rows1), 0) == ggroups[...] + place, 1.0, 0.0).astype(BF16)
    gplain[...] = jnp.where(iota((T, rows1), 0) == ggroups[...], 1.0, 0.0).astype(BF16)
    one_hot_rows(gsel, gsends, nb1)

    table = mm(gagg[...].astype(F32) * gweights[...], gsel[...])
    for side in range(2):
        hp_out[side, 0] = table[:, side * halo1 : (side + 1) * halo1]
        hp_out[side, 1] = jnp.zeros((T, halo1), F32)
    for load in loads:
        load.wait()
    prepare(gtiles, gcols, ghi, glo, gscale, nb1)

    @pl.loop(0, nb1)
    def _(b):
        at = pl.ds(pl.multiple_of(b * T, T), T)
        w = split(gplain[:share, at].astype(F32) * gweights[:, at])
        r = joined(jnp.dot(w, ghi[b, :, T:], preferred_element_type=F32)) + jnp.dot(
            w[:share], glo[b, :, T:], preferred_element_type=F32
        )
        for k in (1, 2):
            for i in range(2 * h1):
                side, s = i // h1, i % h1
                hit = jnp.where(gcols(k, b) == nb1 + i, 1.0, 0.0)
                span = slice(s * T, (s + 1) * T)
                hp_out[side, 1, :share, span] = (
                    hp_out[side, 1, :share, span] + hit * r[:, (k - 1) * T : k * T]
                )

    def hp_copy(side, dev):
        return pltpu.make_async_remote_copy(
            src_ref=hp_out.at[side], dst_ref=hp_in.at[1 - side],
            send_sem=hp_send.at[0, side], recv_sem=hp_recv.at[0, 1 - side],
            device_id=dev, device_id_type=MESH,
        )

    hp_pair = (hp_copy(0, lower_g), hp_copy(1, upper_g))
    start(hp_pair, g_lower, g_upper)
    prepare(ctiles, ccols, chi, clo, cscale, nb2)

    per = T // share
    piece = nrhs // per
    lane = iota((piece, T), 1)

    def packed_part(part):
        out = part[:piece]
        for k in range(1, per):
            out = out + pltpu.roll(part[k * piece : (k + 1) * piece], k * share, 1)
        return out

    def coarse_block(it, c):
        rows = []
        for k in range(per):
            total = jnp.zeros((piece, T), F32)
            for r in range(per):
                shift = ((r - k) * share) % T
                g = c * per + r
                got = cparts[it, g, :piece]
                if g > 0:
                    got = got + cparts[it, g - 1, 2 * piece :]
                if g < ng - 1:
                    got = got + cparts[it, g + 1, piece : 2 * piece]
                if shift:
                    got = pltpu.roll(got, shift, 1)
                total = jnp.where((lane >= r * share) & (lane < (r + 1) * share), got, total)
            rows.append(total)
        return jnp.concatenate(rows, axis=0)

    for it in range(ITERS):
        base = 3 * it
        left = res_out[...] - (fine_apply(base) if it == 0 else fy[...])
        lowered = mm_nt(left * fweights[...], fagg[...])
        for s in range(ob1):
            gathered[it, mem * ob1 + s] = lowered[:, s * T : (s + 1) * T]
        run(spread_copies(gathered, it, mem, ob1, ag_send, ag_recv, "mem"))
        b1 = jnp.concatenate([gathered[it, b] for b in range(nb1)], axis=1)
        first = gscale[...] * b1
        picked = group_send(first, it)
        put_own(first, gext, nb1)
        for s in range(2 * h1):
            gext[nb1 + s] = jnp.zeros((2 * nrhs, T), BF16)
        apply_own(gext, ghi, glo, gy, nb1)
        apply_rest(gext, gcols, ghi, glo, gy, nb1)
        left = b1 - gy[...]
        cparts[it, grp, :piece] = packed_part(mm_nt(left * gweights[...], gplain[...]))
        if it == 0:
            finish(hp_pair, g_lower, g_upper)
            for side in range(2):
                for which in range(2):
                    hp_hi[side, which] = high_part(hp_in[side, which])
                    hp_lo[side, which] = low_part(hp_in[side, which])
        for side in range(2):
            given = split(picked[:, side * halo1 : (side + 1) * halo1])
            felt = joined(dot_nt(given, hp_hi[side, 1])) + dot_nt(given[:nrhs], hp_lo[side, 1])
            cparts[it, grp, (side + 1) * piece : (side + 2) * piece] = packed_part(-felt)
        run(spread_copies(cparts, it, grp, 1, cg_send, cg_recv, "grp"))
        b2 = jnp.concatenate([coarse_block(it, c) for c in range(nb2)], axis=1)
        x2 = cscale[...] * b2
        put_own(x2, cext, nb2)
        apply_own(cext, chi, clo, cy, nb2)
        apply_rest(cext, ccols, chi, clo, cy, nb2)
        cy[...] = x2 + cscale[...] * (b2 - cy[...])
        raised = cy[:, pl.ds(pl.multiple_of(cblock * T, T), T)]
        x1v = first + gweights[...] * mm(raised, gagg[...])
        put_own(x1v, gext, nb1)
        finish(g_pair(it), g_lower, g_upper)
        for side in range(2):
            other = jnp.clip(grp + 2 * side - 1, 0, ng - 1)
            oblock = lax.div(other * share, T)
            far = split(cy[:, pl.ds(pl.multiple_of(oblock * T, T), T)])
            lift = joined(jnp.dot(far, hp_hi[side, 0], preferred_element_type=F32)) + jnp.dot(
                far[:nrhs], hp_lo[side, 0], preferred_element_type=F32
            )
            for s in range(h1):
                at = side * h1 + s
                gext[nb1 + at] = split(gin[it, at] + lift[:, s * T : (s + 1) * T])
        apply_own(gext, ghi, glo, gy, nb1)
        apply_rest(gext, gcols, ghi, glo, gy, nb1)
        x1[...] = x1v + gscale[...] * (b1 - gy[...])
        mine = x1[:, pl.ds(pl.multiple_of(mem * own1, T), own1)]
        x0v = x0[...] + fweights[...] * mm(mine, fagg[...])
        fine_send(x0v, base + 1)
        put_own(x0v, fext, nb0)
        z = x0v + fscale[...] * (res_out[...] - fine_apply(base + 1))
        fine_send(z, base + 2)
        put_own(z, fext, nb0)
        q = fine_apply(base + 2)
        if it == 0:
            zed[...] = z
            img[...] = q
            energy, curvature = reduced(
                [(res_out[...], z), (z, q)], it,
                lambda: fine_send(fscale[...] * img[...], base + 3),
            )
            step = energy / curvature
            sol_out[...] = step * zed[...]
            res = res_out[...] - step * img[...]
            res_out[...] = res
            x0v = fscale[...] * res
            x0[...] = x0v
            put_own(x0v, fext, nb0)
            finish(f_pair(base + 3), has_lower, has_upper)
            for s in range(2 * h0):
                fext[nb0 + s] = split(fin[0, s] - step * fin[base + 3, s])
            apply_own(fext, fhi, flo, fy, nb0)
            apply_rest(fext, fcols, fhi, flo, fy, nb0)
        else:
            fresh, own, one, two = reduced(
                [(res_out[...], z), (z, q), (z, img[...]), (zed[...], q)], it
            )
            ratio = fresh / energy
            curvature = own + ratio * (one + two) + ratio * ratio * curvature
            step = fresh / curvature
            sol_out[...] = sol_out[...] + step * (z + ratio * zed[...])
            res_out[...] = res_out[...] - step * (q + ratio * img[...])


def hand_over(both, sol, res):
    sol[...] = both[0]
    res[...] = both[1]


def shards(
    ng, nm,
    right_side, fine_tiles, fine_columns, fine_sends, fine_weights, fine_groups,
    group_tiles, group_columns, group_sends, group_weights, group_groups,
    coarse_tiles, coarse_columns,
):
    nrhs, rows0 = right_side.shape
    T = fine_tiles.shape[-1]
    nb0, nb1, nb2 = fine_tiles.shape[0], group_tiles.shape[0], coarse_tiles.shape[0]
    rows1, rows2 = nb1 * T, nb2 * T
    h0, h1 = fine_sends.shape[1] // T, group_sends.shape[1] // T
    own1 = rows0 // AGG1
    vm, dma = pltpu.VMEM, pltpu.SemaphoreType.DMA
    scratch = [
        vm((nb0, T, 3 * T), BF16), vm((nb0, T, 3 * T), BF16),
        vm((nb1, T, 3 * T), BF16), vm((nb1, T, 3 * T), BF16),
        vm((nb2, T, 3 * T), BF16), vm((nb2, T, 3 * T), BF16),
        vm((1, rows0), F32), vm((1, rows1), F32), vm((1, rows2), F32),
        vm(group_tiles.shape, F32), vm(coarse_tiles.shape, F32),
        vm((rows0, 2 * h0 * T), BF16), vm((rows1, 2 * h1 * T), BF16),
        vm((own1, rows0), BF16), vm((T, rows1), BF16), vm((T, rows1), BF16),
        vm((2, 2, T, h1 * T), F32), vm((2, 2, T, h1 * T), F32),
        vm((2, 2, T, h1 * T), BF16), vm((2, 2, T, h1 * T), BF16),
        vm((nb0 + 2 * h0, 2 * nrhs, T), BF16),
        vm((nb1 + 2 * h1, 2 * nrhs, T), BF16),
        vm((nb2, 2 * nrhs, T), BF16),
        vm((nrhs, rows0), F32), vm((nrhs, rows1), F32), vm((nrhs, rows2), F32),
        vm((nrhs, rows0), F32), vm((nrhs, rows1), F32),
        vm((nrhs, rows0), F32), vm((nrhs, rows0), F32),
        vm((3 * ITERS, 2 * h0, nrhs, T), F32), vm((3 * ITERS, 2 * h0, nrhs, T), F32),
        vm((ITERS, 2 * h1, nrhs, T), F32), vm((ITERS, 2 * h1, nrhs, T), F32),
        vm((ITERS, nb1, nrhs, T), F32), vm((ITERS, ng, 3 * nrhs * (rows1 // AGG2) // T, T), F32),
        vm((ITERS, nm, 8, T), F32), vm((ITERS, ng, 8, T), F32),
        dma((3 * ITERS, 2)), dma((3 * ITERS, 2)),
        dma((ITERS, 2)), dma((ITERS, 2)),
        dma((ITERS, nm - 1)), dma((ITERS, nm - 1)),
        dma((ITERS, ng - 1)), dma((ITERS, ng - 1)),
        dma((ITERS, nm - 1)), dma((ITERS, nm - 1)),
        dma((ITERS, ng - 1)), dma((ITERS, ng - 1)),
        dma((1, 2)), dma((1, 2)), dma((2,)),
    ]
    in_vm, in_sm = pl.BlockSpec(memory_space=pltpu.VMEM), pl.BlockSpec(memory_space=pltpu.SMEM)
    in_any = pl.BlockSpec(memory_space=pl.ANY)
    out = jax.ShapeDtypeStruct((nrhs, rows0), F32)
    both = pl.pallas_call(
        functools.partial(kernel, ng, nm),
        out_shape=jax.ShapeDtypeStruct((2, nrhs, rows0), F32),
        in_specs=[in_sm] * 3 + [in_vm] * 5 + [in_any] + [in_vm] * 3 + [in_any],
        out_specs=in_vm,
        scratch_shapes=scratch,
        compiler_params=pltpu.CompilerParams(
            collective_id=0, has_side_effects=True, vmem_limit_bytes=60 << 20
        ),
    )(
        fine_columns.T, group_columns.T, coarse_columns,
        right_side, fine_tiles, fine_sends, fine_weights.reshape(1, -1),
        fine_groups.reshape(1, -1), group_tiles, group_sends,
        group_weights.reshape(1, -1), group_groups.reshape(1, -1), coarse_tiles,
    )
    return pl.pallas_call(
        hand_over, out_shape=(out, out), in_specs=[in_vm], out_specs=(in_vm, in_vm)
    )(both)


def solution(mesh):
    both = ("grp", "mem")
    return jax.shard_map(
        functools.partial(shards, mesh.shape["grp"], mesh.shape["mem"]),
        mesh=mesh,
        in_specs=(
            P(None, both), P(both, None, None, None), P(both, None), P(both, None), P(both), P(both),
            P("grp", None, None, None), P("grp", None), P("grp", None), P("grp"), P("grp"),
            P(), P(),
        ),
        out_specs=(P(None, both), P(None, both)),
        check_vma=False,
    )
```
